32 devices in a mesh: member: 2 (over x), block: 16 (over z, y, core).
Axes of the slice: x: 2, y: 2, z: 4, core: 2. Of those that a mesh axis runs over, the one named last changes fastest.
Arguments:
- grid_in: bfloat16 [32768, 128], P(('member', 'block')), parts along dimension 0, may hold values from -6 to 6
- dest_block: int32 [32768, 1], P(('member', 'block')), parts along dimension 0, may hold values from 0 to 15, as said below
- dest_node: int32 [32768], P(('member', 'block')), parts along dimension 0, may hold values from 0 to 255
- neighbour_mask: int32 [8192, 4], P(('member', 'block')), parts along dimension 0, may hold values 0 or 1
- mesh_embed: bfloat16 [8192, 512], P(('member', 'block')), parts along dimension 0, may hold values from -6 to 6
- w_in: bfloat16 [128, 512], replicated, may hold values from -0.5 to 0.5
- in_bias: bfloat16 [512], replicated, may hold values from -3 to 3
- w_grid: bfloat16 [512, 512], replicated, may hold values from -0.25 to 0.25
- w_enc: bfloat16 [512, 512], replicated, may hold values from -0.25 to 0.25
- attn_gain: bfloat16 [2, 512], replicated, may hold values from 0.099609375 to 1.8984375
- w_query: bfloat16 [2, 512, 512], replicated, may hold values from -0.25 to 0.25
- w_key: bfloat16 [2, 512, 512], replicated, may hold values from -0.25 to 0.25
- w_value: bfloat16 [2, 512, 512], replicated, may hold values from -0.25 to 0.25
- w_out: bfloat16 [2, 512, 512], replicated, may hold values from -0.25 to 0.25
- mlp_gain: bfloat16 [2, 512], replicated, may hold values from 0.099609375 to 1.8984375
- w_up: bfloat16 [2, 512, 512], replicated, may hold values from -0.25 to 0.25
- w_down: bfloat16 [2, 512, 512], replicated, may hold values from -0.25 to 0.25
- dec_gain: bfloat16 [512], replicated, may hold values from 0.099609375 to 1.8984375
- w_dec: bfloat16 [512, 512], replicated, may hold values from -0.25 to 0.25
- w_head: bfloat16 [512, 512], replicated, may hold values from -0.25 to 0.25
- w_final: bfloat16 [512, 128], replicated, may hold values from -0.25 to 0.25
Outputs:
- grid_out: bfloat16 [32768, 128], P(('member', 'block')), parts along dimension 0
The draws below stay inside these ranges and needn't reach their ends.
There are 2 independent parts, one for each index of `member`. The reference program is written for one: setup_inputs(seed, part) draws one part's arguments, and reference() takes and returns one part's arrays. A program takes and returns all parts, laid end to end along the dimension named above; an argument that names none is the same for every part. Nothing has to cross between parts.
Inputs may be any that keep to these rules, and one draw needn't show every extreme that they name: `dest_block`: A grid point of block b maps into one of the mesh blocks b-2, b-1, b, b+1, b+2 (modulo 16); within the 1024 rows of one block exactly 512 name one of these five, and the others name fewer.
All inputs are finite; a program needn't handle non-finite values. No bound on the sum of `neighbour_mask` on one device may be relied on, other than what follows from the above.
Results may differ from the reference program's by a relative error of at most 0.014.
Values may be sent and summed in bfloat16 or wider, within the bound.
No kernel may reach another device: no remote copies, remote signals or barrier semaphores. Data moves between devices by JAX's collectives and lax.ppermute only.
A program may use at most 64 MiB of HBM per device.

```python
import jax
import jax.numpy as jnp
from jax import lax

D = 512
IN = 128
HEADS = 8
LAYERS = 2
GRID_DEV = 1024
MESH_DEV = 256
GRID = 16384
N_NODES = 4096
N_BLOCK = 16


def draw_dest_block(key, part):
    key_heavy = jax.random.fold_in(key, 11)
    key_other = jax.random.fold_in(key, 12)
    key_order = jax.random.fold_in(key, 13)
    heavy = jax.random.randint(key_heavy, (N_BLOCK, 1), 0, 5)
    others = jax.random.randint(key_other, (N_BLOCK, GRID_DEV), 1, 5)
    ranks = jax.vmap(lambda k: jax.random.permutation(k, GRID_DEV))(jax.random.split(key_order, N_BLOCK))
    picked = jnp.where(ranks < GRID_DEV // 2, heavy, (heavy + others) % 5)
    blocks = jnp.arange(N_BLOCK, dtype=jnp.int32)[:, None]
    dest = (blocks + picked.astype(jnp.int32) - 2) % N_BLOCK
    return dest.reshape(GRID, 1).astype(jnp.int32)


def place_ends(result, own_key, low, high):
    extent = result.shape
    place = [jax.random.randint(jax.random.fold_in(own_key, axis), (), 0, extent[axis]) for axis in range(len(extent))]
    result = result.at[tuple(place)].set(low)
    longest = extent.index(max(extent))
    place[longest] = (place[longest] + 1) % extent[longest]
    return result.at[tuple(place)].set(high)


def block_levels(own_key, extent, cuts, least, high):
    level, own = 1.0, jax.random.fold_in(own_key, 6)
    for position, blocks in cuts:
        heights = jnp.exp(jax.random.uniform(jax.random.fold_in(own, position), (blocks,), jnp.float32, least / len(cuts), high / len(cuts)))
        level = level * jnp.repeat(heights, extent[position] // blocks).reshape([-1 if axis == position else 1 for axis in range(len(extent))])
    return level


def normal_values(key, extent, deviation, most, cuts=(), kind=jnp.bfloat16):
    array = jax.random.normal(key, extent, jnp.float32) * deviation
    if len(cuts) > 0:
        array = block_levels(key, extent, cuts, -0.22, 0.18) * array
    return jnp.clip(array, min=-most, max=most).astype(kind)


def setup_inputs(seed: int = 0, part: int = 0) -> dict:
    seeds = jax.random.split(jax.random.key(seed), 22)
    own_keys = jax.random.split(jax.random.fold_in(seeds[21], part), 22)
    return {
        "grid_in": normal_values(own_keys[0], (GRID, IN), 1.0, 6.0, ((0, 16),)),
        "dest_block": draw_dest_block(jax.random.fold_in(jax.random.fold_in(seeds[21], part), 71), part),
        "dest_node": place_ends(jax.random.randint(own_keys[2], (GRID,), 0, MESH_DEV), jax.random.fold_in(own_keys[2], 1), 0, MESH_DEV - 1).astype(jnp.int32),
        "neighbour_mask": place_ends((jax.random.randint(own_keys[3], (N_NODES, 4), 0, 4) < 3).astype(jnp.int32), jax.random.fold_in(own_keys[3], 1), 0, 1),
        "mesh_embed": normal_values(own_keys[4], (N_NODES, D), 1.0, 6.0, ((0, 16),)),
        "w_in": normal_values(seeds[5], (IN, D), IN ** -0.5, 0.5),
        "in_bias": normal_values(seeds[6], (D,), 0.5, 3.0),
        "w_grid": normal_values(seeds[7], (D, D), D ** -0.5, 0.25),
        "w_enc": normal_values(seeds[8], (D, D), D ** -0.5, 0.25),
        "attn_gain": jnp.clip(1.0 + 0.18 * jax.random.normal(seeds[9], (LAYERS, D), jnp.float32), 0.099609375, 1.8984375).astype(jnp.bfloat16),
        "w_query": normal_values(seeds[10], (LAYERS, D, D), D ** -0.5, 0.25),
        "w_key": normal_values(seeds[11], (LAYERS, D, D), D ** -0.5, 0.25),
        "w_value": normal_values(seeds[12], (LAYERS, D, D), D ** -0.5, 0.25),
        "w_out": normal_values(seeds[13], (LAYERS, D, D), D ** -0.5, 0.25),
        "mlp_gain": jnp.clip(1.0 + 0.18 * jax.random.normal(seeds[14], (LAYERS, D), jnp.float32), 0.099609375, 1.8984375).astype(jnp.bfloat16),
        "w_up": normal_values(seeds[15], (LAYERS, D, D), D ** -0.5, 0.25),
        "w_down": normal_values(seeds[16], (LAYERS, D, D), D ** -0.5, 0.25),
        "dec_gain": jnp.clip(1.0 + 0.18 * jax.random.normal(seeds[17], (D,), jnp.float32), 0.099609375, 1.8984375).astype(jnp.bfloat16),
        "w_dec": normal_values(seeds[18], (D, D), D ** -0.5, 0.25),
        "w_head": normal_values(seeds[19], (D, D), D ** -0.5, 0.25),
        "w_final": normal_values(seeds[20], (D, IN), D ** -0.5, 0.25),
    }


def rms_norm(values, gain):
    return values * lax.rsqrt(lax.optimization_barrier(jnp.mean(values * values, axis=-1, keepdims=True)) + 1e-06) * gain.astype(jnp.float32)

def attend_all(query_rows, key_rows, value_rows, neighbour_mask):
    head_dim = D // HEADS
    query_blocks = query_rows.reshape(N_BLOCK, MESH_DEV, HEADS, head_dim)
    key_blocks = key_rows.reshape(N_BLOCK, MESH_DEV, HEADS, head_dim)
    value_blocks = value_rows.reshape(N_BLOCK, MESH_DEV, HEADS, head_dim)
    mask_blocks = neighbour_mask.reshape(N_BLOCK, MESH_DEV, 4)
    offsets = jnp.arange(-2, 3, dtype=jnp.int32)

    def single(block_index):
        near_blocks = (block_index + offsets) % N_BLOCK
        keys_near = key_blocks[near_blocks].reshape(5 * MESH_DEV, HEADS, head_dim).astype(jnp.float32)
        values_near = value_blocks[near_blocks].reshape(5 * MESH_DEV, HEADS, head_dim).astype(jnp.float32)
        queries = query_blocks[block_index].astype(jnp.float32)
        own_mask = mask_blocks[block_index]
        allowed = jnp.concatenate([own_mask[:, :2], jnp.ones((MESH_DEV, 1), jnp.int32), own_mask[:, 2:]], axis=1) > 0
        scores = jnp.einsum('qhd,khd->hqk', queries, keys_near) * head_dim ** (-0.5)
        scores = jnp.where(allowed[None, :, :, None], scores.reshape(HEADS, MESH_DEV, 5, MESH_DEV), -jnp.inf)
        scores = scores.reshape(HEADS, MESH_DEV, 5 * MESH_DEV)
        largest = lax.optimization_barrier(jnp.max(scores, axis=-1, keepdims=True))
        exponent = jnp.exp(scores - largest)
        softmax_weights = (exponent / lax.optimization_barrier(jnp.sum(exponent, axis=-1, keepdims=True))).astype(jnp.bfloat16)
        attended = jnp.einsum('hqk,khd->qhd', softmax_weights.astype(jnp.float32), values_near)
        return attended.astype(jnp.bfloat16).reshape(MESH_DEV, D)
    return lax.map(single, jnp.arange(N_BLOCK, dtype=jnp.int32)).reshape(N_NODES, D)

def reference(grid_in, dest_block, dest_node, neighbour_mask, mesh_embed, w_in, in_bias, w_grid, w_enc, attn_gain, w_query, w_key, w_value, w_out, mlp_gain, w_up, w_down, dec_gain, w_dec, w_head, w_final):
    grid_hidden = jax.nn.silu(jnp.dot(grid_in, w_in, preferred_element_type=jnp.float32) + in_bias.astype(jnp.float32)).astype(jnp.bfloat16)
    grid_feat = jnp.dot(grid_hidden, w_grid, preferred_element_type=jnp.float32).astype(jnp.bfloat16)
    target = (dest_block[:, 0] * MESH_DEV + dest_node).astype(jnp.int32)
    summed = jnp.zeros((N_NODES, D), jnp.float32).at[target].add(grid_feat.astype(jnp.float32))
    counts = jnp.zeros((N_NODES,), jnp.float32).at[target].add(jnp.ones((GRID,), jnp.float32))
    mean_rows = (summed / jnp.maximum(counts, 1.0)[:, None]).astype(jnp.bfloat16)
    mesh_state = mesh_embed.astype(jnp.float32) + jnp.dot(mean_rows, w_enc, preferred_element_type=jnp.float32)
    for layer_index in range(LAYERS):
        normed = rms_norm(mesh_state, attn_gain[layer_index]).astype(jnp.bfloat16)
        query_rows = jnp.dot(normed, w_query[layer_index], preferred_element_type=jnp.float32).astype(jnp.bfloat16)
        key_rows = jnp.dot(normed, w_key[layer_index], preferred_element_type=jnp.float32).astype(jnp.bfloat16)
        value_rows = jnp.dot(normed, w_value[layer_index], preferred_element_type=jnp.float32).astype(jnp.bfloat16)
        attended = attend_all(query_rows, key_rows, value_rows, neighbour_mask)
        mesh_state = mesh_state + jnp.dot(attended, w_out[layer_index], preferred_element_type=jnp.float32)
        normed_second = rms_norm(mesh_state, mlp_gain[layer_index]).astype(jnp.bfloat16)
        up_hidden = jax.nn.silu(jnp.dot(normed_second, w_up[layer_index], preferred_element_type=jnp.float32)).astype(jnp.bfloat16)
        mesh_state = mesh_state + jnp.dot(up_hidden, w_down[layer_index], preferred_element_type=jnp.float32)
    decoded = rms_norm(mesh_state, dec_gain).astype(jnp.bfloat16)
    gathered = decoded[target]
    grid_mix = (grid_feat.astype(jnp.float32) + jnp.dot(gathered, w_dec, preferred_element_type=jnp.float32)).astype(jnp.bfloat16)
    head_rows = jax.nn.silu(jnp.dot(grid_mix, w_head, preferred_element_type=jnp.float32)).astype(jnp.bfloat16)
    return jnp.dot(head_rows, w_final, preferred_element_type=jnp.float32).astype(jnp.bfloat16)
```

```python
import functools

import jax
import jax.numpy as jnp
from jax import lax
from jax.experimental import pallas as pl
from jax.experimental.pallas import tpu as pltpu
from jax.sharding import PartitionSpec as P

HEADS = 8
LAYERS = 2
LANES = 128
BF16 = jnp.bfloat16
F32 = jnp.float32
LOG2E = 1.4426950408889634
FAR = 1e30


OFFSETS = {"own": 0, "pair": 1, "near": -1, "wide": 2, "far": -2}


def send(value, step_even, step_odd):
    count = lax.axis_size("block")
    pairs = [
        (source, (source + (step_even if source % 2 == 0 else step_odd)) % count)
        for source in range(count)
    ]
    return lax.ppermute(value, "block", pairs)


def spread(value):
    near = send(value, -1, 1)
    far = send(value, 2, -2)
    pair = send(value, 1, -1)
    wide = send(near, 1, -1)
    return pair, near, wide, far


def dot(left, right):
    return lax.dot_general(left, right, (((1,), (0,)), ((), ())), preferred_element_type=F32)


def dot_t(left, right):
    return lax.dot_general(left, right, (((1,), (1,)), ((), ())), preferred_element_type=F32)


def silu(values):
    half = 0.5 * values
    return half * (jnp.tanh(half) + 1.0)


def rms(values, gain):
    mean = jnp.mean(values * values, axis=-1, keepdims=True)
    return values * lax.rsqrt(mean + 1e-06) * gain


def codes(packed_ref, grid_rows, sign, offset):
    id_rows = grid_rows // LANES
    node = packed_ref[pl.ds(grid_rows, id_rows), :].astype(F32)
    step = packed_ref[pl.ds(grid_rows + id_rows, id_rows), :].astype(F32) * sign
    return jnp.where(step == float(offset), node, -1.0)


def gather_sums(packed_ref, grid_rows, sign, offset, w_in, bias, total, count):
    mesh_rows = total.shape[0]
    hidden = silu(dot(packed_ref[pl.ds(0, grid_rows), :], w_in) + bias).astype(BF16)
    code = codes(packed_ref, grid_rows, sign, -offset).astype(jnp.int32)
    nodes = lax.broadcasted_iota(jnp.int32, (mesh_rows, LANES), 0)
    pieces = []
    for row in range(grid_rows // LANES):
        hit = jnp.where(nodes == code[row : row + 1, :], 1.0, 0.0)
        count = count + hit
        pieces.append(hit.astype(BF16))
    total = total + dot(jnp.concatenate(pieces, axis=1), hidden)
    return hidden, total, count


def encode_first_kernel(sign_ref, own_ref, pair_ref, w_in_ref, bias_ref, w_grid_ref, total_ref, count_ref, feat_ref):
    sign = sign_ref[0].astype(F32)
    grid_rows = feat_ref.shape[0]
    bias = bias_ref[...].astype(F32)
    total, count = jnp.zeros(total_ref.shape, F32), jnp.zeros(count_ref.shape, F32)
    hidden, total, count = gather_sums(own_ref, grid_rows, sign, 0, w_in_ref[...], bias, total, count)
    feat_ref[...] = dot(hidden, w_grid_ref[...]).astype(BF16)
    _, total, count = gather_sums(pair_ref, grid_rows, sign, OFFSETS["pair"], w_in_ref[...], bias, total, count)
    total_ref[...] = total
    count_ref[...] = count


def encode_mid_kernel(grid_rows, sign_ref, near_ref, wide_ref, w_in_ref, bias_ref, total_in, count_in, total_ref, count_ref):
    sign = sign_ref[0].astype(F32)
    bias = bias_ref[...].astype(F32)
    total, count = total_in[...], count_in[...]
    for ref, role in ((near_ref, "near"), (wide_ref, "wide")):
        _, total, count = gather_sums(ref, grid_rows, sign, OFFSETS[role], w_in_ref[...], bias, total, count)
    total_ref[...] = total
    count_ref[...] = count


def encode_last_kernel(
    grid_rows, sign_ref, far_ref, w_in_ref, bias_ref, total_in, count_in, w_grid_ref, w_enc_ref, embed_ref, gain_ref,
    state_ref, normed_ref,
):
    sign = sign_ref[0].astype(F32)
    bias = bias_ref[...].astype(F32)
    _, total, count = gather_sums(
        far_ref, grid_rows, sign, OFFSETS["far"], w_in_ref[...], bias, total_in[...], count_in[...]
    )
    counts = jnp.sum(count, axis=1, keepdims=True)
    mean_hidden = (total / jnp.maximum(counts, 1.0)).astype(BF16)
    mean_rows = dot(mean_hidden, w_grid_ref[...]).astype(BF16)
    state = embed_ref[...].astype(F32) + dot(mean_rows, w_enc_ref[...])
    state_ref[...] = state
    normed_ref[...] = rms(state, gain_ref[...].astype(F32)).astype(BF16)


def column(values, index):
    return values[:, index : index + 1]


def attend_blocks(head_dim, pair_index, query_pair, keys, values, allowed, carry):
    rows = query_pair.shape[0]
    low = lax.broadcasted_iota(jnp.int32, (rows, LANES), 1) < head_dim
    lanes = slice(pair_index * LANES, (pair_index + 1) * LANES)
    zero = jnp.zeros_like(query_pair)
    queries = (jnp.where(low, query_pair, zero), jnp.where(low, zero, query_pair))
    scores = [[dot_t(query, key[:, lanes]) * LOG2E for key in keys] for query in queries]
    tops, shifts = [], []
    for half in range(2):
        top = None if carry is None else column(carry[2], half * head_dim)
        for score, allow in zip(scores[half], allowed):
            most = jnp.max(score, axis=1, keepdims=True)
            if allow is not None:
                most = jnp.where(allow, most, -FAR)
            top = most if top is None else jnp.maximum(top, most)
        tops.append(top)
    ones = jnp.ones((keys[0].shape[0], LANES), BF16)
    sums = [None, None]
    for half in range(2):
        for score, allow, value in zip(scores[half], allowed, values):
            shift = tops[half] if allow is None else jnp.where(allow, tops[half], FAR)
            weights = jnp.exp2(score - shift).astype(BF16)
            part = dot(weights, jnp.concatenate([value[:, lanes], ones], axis=1))
            sums[half] = part if sums[half] is None else sums[half] + part
    acc = jnp.where(low, sums[0][:, :LANES], sums[1][:, :LANES])
    norm = jnp.where(low, sums[0][:, LANES:], sums[1][:, LANES:])
    top = jnp.where(low, tops[0], tops[1])
    if carry is not None:
        fade = jnp.exp2(carry[2] - top)
        acc = carry[0] * fade + acc
        norm = carry[1] * fade + norm
    return acc, norm, top


def attend_mid_kernel(
    head_dim, own_ref, pair_ref, near_ref, wide_ref, mask_ref, w_query_ref, w_key_ref, w_value_ref,
    query_ref, acc_ref, norm_ref, top_ref,
):
    mask = mask_ref[...]
    allowed = [None] + [column(mask, index) > 0 for index in (2, 1, 3)]
    query = dot(own_ref[...], w_query_ref[...]).astype(BF16)
    query = query * jnp.asarray(head_dim**-0.5, BF16)
    query_ref[...] = query
    blocks = [own_ref, pair_ref, near_ref, wide_ref]
    keys = [dot(block[...], w_key_ref[...]).astype(BF16) for block in blocks]
    values = [dot(block[...], w_value_ref[...]).astype(BF16) for block in blocks]
    for index in range(query.shape[1] // LANES):
        lanes = slice(index * LANES, (index + 1) * LANES)
        acc, norm, top = attend_blocks(head_dim, index, query[:, lanes], keys, values, allowed, None)
        acc_ref[:, lanes] = acc
        norm_ref[:, lanes] = norm
        top_ref[:, lanes] = top


def attend_last_kernel(
    head_dim, far_ref, mask_ref, w_key_ref, w_value_ref, query_ref, acc_ref, norm_ref, top_ref,
    state_in, w_out_ref, mlp_gain_ref, w_up_ref, w_down_ref, next_gain_ref, state_ref, normed_ref,
):
    allowed = [column(mask_ref[...], 0) > 0]
    keys = [dot(far_ref[...], w_key_ref[...]).astype(BF16)]
    values = [dot(far_ref[...], w_value_ref[...]).astype(BF16)]
    pieces = []
    for index in range(query_ref.shape[1] // LANES):
        lanes = slice(index * LANES, (index + 1) * LANES)
        carry = (acc_ref[:, lanes], norm_ref[:, lanes], top_ref[:, lanes])
        acc, norm, _ = attend_blocks(head_dim, index, query_ref[:, lanes], keys, values, allowed, carry)
        pieces.append((acc / norm).astype(BF16))
    state = state_in[...] + dot(jnp.concatenate(pieces, axis=1), w_out_ref[...])
    normed = rms(state, mlp_gain_ref[...].astype(F32)).astype(BF16)
    up_hidden = silu(dot(normed, w_up_ref[...])).astype(BF16)
    state = state + dot(up_hidden, w_down_ref[...])
    state_ref[...] = state
    normed_ref[...] = rms(state, next_gain_ref[...].astype(F32)).astype(BF16)


def pick_rows(own_ids_ref, sign, role, decoded):
    id_rows = own_ids_ref.shape[0] // 2
    code = jnp.transpose(role_codes(own_ids_ref, sign, role))
    nodes = lax.broadcasted_iota(jnp.int32, (LANES, decoded.shape[0]), 1).astype(F32)
    hits = [jnp.where(nodes == column(code, row), 1.0, 0.0).astype(BF16) for row in range(id_rows)]
    return dot(jnp.concatenate(hits, axis=0), decoded)


def role_codes(ids_ref, sign, role):
    id_rows = ids_ref.shape[0] // 2
    node = ids_ref[pl.ds(0, id_rows), :].astype(F32)
    step = ids_ref[pl.ds(id_rows, id_rows), :].astype(F32) * sign
    return jnp.where(step == float(OFFSETS[role]), node, -1.0)


def decode_mid_kernel(sign_ref, ids_ref, own_ref, pair_ref, near_ref, wide_ref, feat_ref, w_dec_ref, mix_ref):
    sign = sign_ref[0].astype(F32)
    rows = None
    for ref, role in ((own_ref, "own"), (pair_ref, "pair"), (near_ref, "near"), (wide_ref, "wide")):
        part = pick_rows(ids_ref, sign, role, ref[...])
        rows = part if rows is None else rows + part
    mix_ref[...] = feat_ref[...].astype(F32) + dot(rows.astype(BF16), w_dec_ref[...])


def decode_last_kernel(sign_ref, ids_ref, far_ref, mix_ref, w_dec_ref, w_head_ref, w_final_ref, out_ref):
    sign = sign_ref[0].astype(F32)
    rows = pick_rows(ids_ref, sign, "far", far_ref[...]).astype(BF16)
    mix = (mix_ref[...] + dot(rows, w_dec_ref[...])).astype(BF16)
    head_rows = silu(dot(mix, w_head_ref[...])).astype(BF16)
    out_ref[...] = dot(head_rows, w_final_ref[...]).astype(BF16)


def call(kernel, outs, flops, smem=False):
    def run(*operands):
        specs = [pl.BlockSpec(memory_space=pltpu.VMEM) for _ in operands]
        if smem:
            specs[0] = pl.BlockSpec(memory_space=pltpu.SMEM)
        size = sum(o.size * o.dtype.itemsize for o in operands) + sum(
            o.size * o.dtype.itemsize for o in outs
        )
        return pl.pallas_call(
            kernel,
            out_shape=outs,
            in_specs=specs,
            out_specs=[pl.BlockSpec(memory_space=pltpu.VMEM) for _ in outs],
            cost_estimate=pl.CostEstimate(flops=flops, bytes_accessed=size, transcendentals=0),
        )(*operands)

    return run


def shape(rows, columns, dtype):
    return jax.ShapeDtypeStruct((rows, columns), dtype)


def body(
    grid_in, dest_block, dest_node, neighbour_mask, mesh_embed, w_in, in_bias, w_grid, w_enc, attn_gain, w_query,
    w_key, w_value, w_out, mlp_gain, w_up, w_down, dec_gain, w_dec, w_head, w_final,
):
    block_count = lax.axis_size("block")
    me = lax.axis_index("block")
    grid_rows, channels = grid_in.shape
    mesh_rows, width = mesh_embed.shape
    out_width = w_final.shape[1]
    head_dim = width // HEADS
    even = me % 2 == 0
    sign = jnp.where(even, 1, -1).astype(jnp.int32).reshape(1)
    relative = (dest_block[:, 0] - me) % block_count
    relative = jnp.where(relative > block_count // 2, relative - block_count, relative)
    ids = jnp.concatenate(
        [dest_node.reshape(-1, LANES).astype(BF16), relative.reshape(-1, LANES).astype(BF16)], axis=0
    )
    packed = jnp.concatenate([grid_in, ids], axis=0)
    mask = jnp.where(even, neighbour_mask, neighbour_mask[:, ::-1])
    bias = in_bias.reshape(1, -1)

    pair, near, wide, far = spread(packed)
    sums = [shape(mesh_rows, width, F32), shape(mesh_rows, LANES, F32)]
    block_flops = 2 * grid_rows * width * (channels + mesh_rows)
    total, count, feat = call(
        encode_first_kernel, sums + [shape(grid_rows, width, BF16)], 3 * block_flops, True
    )(sign, packed, pair, w_in, bias, w_grid)
    total, count = call(functools.partial(encode_mid_kernel, grid_rows), sums, 2 * block_flops, True)(
        sign, near, wide, w_in, bias, total, count
    )
    states = [shape(mesh_rows, width, F32), shape(mesh_rows, width, BF16)]
    state, normed = call(functools.partial(encode_last_kernel, grid_rows), states, block_flops, True)(
        sign, far, w_in, bias, total, count, w_grid, w_enc, mesh_embed, attn_gain[0:1]
    )
    gains = [attn_gain[layer : layer + 1] for layer in range(1, LAYERS)] + [dec_gain.reshape(1, -1)]
    carries = [shape(mesh_rows, width, BF16)] + [shape(mesh_rows, width, F32)] * 3
    attend_flops = 4 * mesh_rows * width * (width + mesh_rows) * 2
    for layer in range(LAYERS):
        pair, near, wide, far = spread(normed)
        query, acc, norm, top = call(functools.partial(attend_mid_kernel, head_dim), carries, 4 * attend_flops)(
            normed, pair, near, wide, mask, w_query[layer], w_key[layer], w_value[layer]
        )
        state, normed = call(functools.partial(attend_last_kernel, head_dim), states, 2 * attend_flops)(
            far, mask, w_key[layer], w_value[layer], query, acc, norm, top, state,
            w_out[layer], mlp_gain[layer : layer + 1], w_up[layer], w_down[layer], gains[layer],
        )
    pair, near, wide, far = spread(normed)
    (mix,) = call(
        decode_mid_kernel, [shape(grid_rows, width, F32)], 2 * grid_rows * width * (4 * mesh_rows + width), True
    )(sign, ids, normed, pair, near, wide, feat, w_dec)
    (grid_out,) = call(
        decode_last_kernel, [shape(grid_rows, out_width, BF16)], 2 * grid_rows * width * 3 * width, True
    )(sign, ids, far, mix, w_dec, w_head, w_final)
    return grid_out


def solution(mesh):
    split = P(("member", "block"), None)
    placed = (split, split, P(("member", "block")), split, split) + (P(),) * 16
    return jax.shard_map(body, mesh=mesh, in_specs=placed, out_specs=split, check_vma=False)
```

```python
import functools

import jax
import jax.numpy as jnp
import numpy as np
from jax import lax
from jax.experimental import pallas as pl
from jax.experimental.pallas import tpu as pltpu
from jax.sharding import PartitionSpec as P

HEADS = 8
LAYERS = 2
LANES = 128
BF16 = jnp.bfloat16
F32 = jnp.float32
LOG2E = 1.4426950408889634
FAR = 1e30
KERNEL_VMEM = 24 * 1024 * 1024


OFFSETS = {"own": 0, "pair": 1, "near": -1, "wide": 2, "far": -2}


def send(value, step_even, step_odd):
    count = lax.axis_size("block")
    pairs = [
        (source, (source + (step_even if source % 2 == 0 else step_odd)) % count)
        for source in range(count)
    ]
    return lax.ppermute(value, "block", pairs)


def spread(value):
    near = send(value, -1, 1)
    far = send(value, 2, -2)
    pair = send(value, 1, -1)
    wide = send(near, 1, -1)
    return pair, near, wide, far


def dot(left, right):
    return lax.dot_general(left, right, (((1,), (0,)), ((), ())), preferred_element_type=F32)


def dot_t(left, right):
    return lax.dot_general(left, right, (((1,), (1,)), ((), ())), preferred_element_type=F32)


def silu(values):
    half = 0.5 * values
    return half * (jnp.tanh(half) + 1.0)


def rms(values, gain):
    mean = jnp.mean(values * values, axis=-1, keepdims=True)
    return values * lax.rsqrt(mean + 1e-06) * gain


def parity(me_ref):
    return lax.rem(me_ref[0], 2)


def offset_of(role, odd):
    return OFFSETS[role] * (1 - 2 * odd)


def pack_kernel(block_count, me_ref, grid_ref, block_ref, node_ref, packed_ref, ids_ref):
    grid_rows = grid_ref.shape[0]
    relative = block_ref[...] - me_ref[0]
    relative = jnp.where(relative > 2, relative - block_count, relative)
    relative = jnp.where(relative < -2, relative + block_count, relative)
    ids = jnp.concatenate([node_ref[...].astype(F32), relative.astype(F32)], axis=0).astype(BF16)
    ids_ref[...] = ids
    packed_ref[pl.ds(0, grid_rows), :] = grid_ref[...]
    packed_ref[pl.ds(grid_rows, ids.shape[0]), :] = ids


def node_sums(packed_ref, grid_rows, offset, w_in, bias, total, count):
    mesh_rows = total.shape[0]
    id_rows = grid_rows // LANES
    hidden = silu(dot(packed_ref[pl.ds(0, grid_rows), :], w_in) + bias).astype(BF16)
    ids = packed_ref[pl.ds(grid_rows, 2 * id_rows), :].astype(F32)
    code = jnp.where(ids[id_rows:] == -offset.astype(F32), ids[:id_rows], -1.0).astype(jnp.int32)
    nodes = lax.broadcasted_iota(jnp.int32, (mesh_rows, LANES), 0)
    pieces = []
    for row in range(id_rows):
        hit = jnp.where(nodes == code[row : row + 1, :], 1.0, 0.0)
        count = count + hit
        pieces.append(hit.astype(BF16))
    total = total + dot(jnp.concatenate(pieces, axis=1), hidden)
    return hidden, total, count


def encode_kernel(roles, grid_rows, me_ref, *refs):
    odd = parity(me_ref)
    blocks, refs = refs[: len(roles)], refs[len(roles) :]
    w_in_ref, bias_ref, refs = refs[0], refs[1], refs[2:]
    bias = bias_ref[...].astype(F32)
    first, last = roles[0] == "own", roles[-1] == "far"
    if first:
        w_grid_ref, mask_ref, total_ref, count_ref, feat_ref, gate_ref = refs
        total, count = jnp.zeros(total_ref.shape, F32), jnp.zeros(count_ref.shape, F32)
        closed = jnp.where(mask_ref[...] > 0, 0.0, -FAR)
        closed = jnp.concatenate([closed, jnp.zeros((LANES - closed.shape[0], closed.shape[1]), F32)], axis=0)
        gate_ref[...] = jnp.transpose(closed).astype(BF16)
    elif last:
        total_in, count_in, w_grid_ref, w_enc_ref, embed_ref, gain_ref, state_ref, normed_ref = refs
        total, count = total_in[...], count_in[...]
    else:
        total_in, count_in, total_ref, count_ref = refs
        total, count = total_in[...], count_in[...]
    for role, ref in zip(roles, blocks):
        hidden, total, count = node_sums(
            ref, grid_rows, offset_of(role, odd), w_in_ref[...], bias, total, count
        )
        if role == "own":
            feat_ref[...] = dot(hidden, w_grid_ref[...]).astype(BF16)
    if not last:
        total_ref[...] = total
        count_ref[...] = count
        return
    counts = jnp.sum(count, axis=1, keepdims=True)
    mean_hidden = (total / jnp.maximum(counts, 1.0)).astype(BF16)
    mean_rows = dot(mean_hidden, w_grid_ref[...]).astype(BF16)
    state = embed_ref[...].astype(F32) + dot(mean_rows, w_enc_ref[...])
    state_ref[...] = state
    normed_ref[...] = rms(state, gain_ref[0:1, :].astype(F32)).astype(BF16)


def key_gate(role, odd, rows):
    lane = lax.broadcasted_iota(jnp.int32, (rows, LANES), 1)
    if role == "own":
        return jnp.zeros((rows, LANES), BF16)
    offset = OFFSETS[role]
    place = offset + 2 if offset < 0 else offset + 1
    place = place + odd * (3 - 2 * place)
    return jnp.where(lane == place, 1.0, 0.0).astype(BF16)


def attend_kernel(roles, layer, head_dim, me_ref, *refs):
    odd = parity(me_ref)
    blocks, refs = refs[: len(roles)], refs[len(roles) :]
    gate_ref, w_key_ref, w_value_ref, refs = refs[0], refs[1], refs[2], refs[3:]
    first, last = roles[0] == "own", roles[-1] == "far"
    rows, width = blocks[0].shape
    if first:
        w_query_ref, query_ref, acc_ref, norm_ref, top_ref = refs
        query = dot(blocks[0][...], w_query_ref[layer]) * (head_dim**-0.5 * LOG2E)
        query = query.astype(BF16)
        query_ref[...] = query
    elif last:
        (query_in, acc_in, norm_in, top_in, state_in, w_out_ref, mlp_gain_ref, w_up_ref, w_down_ref,
         next_gain_ref, state_ref, normed_ref) = refs
        query = query_in[...]
    else:
        query_in, acc_in, norm_in, top_in, acc_ref, norm_ref, top_ref = refs
        query = query_in[...]
    near = jnp.concatenate([block[...] for block in blocks], axis=0)
    keys = dot(near, w_key_ref[layer]).astype(BF16)
    values = dot(near, w_value_ref[layer]).astype(BF16)
    gates = jnp.concatenate([key_gate(role, odd, rows) for role in roles], axis=0)
    ones = jnp.ones(gates.shape, BF16)
    gate = gate_ref[...]
    low = lax.broadcasted_iota(jnp.int32, (rows, LANES), 1) < head_dim
    pieces = []
    for index in range(width // LANES):
        lanes = slice(index * LANES, (index + 1) * LANES)
        part = query[:, lanes]
        zero = jnp.zeros_like(part)
        queries = jnp.concatenate(
            [
                jnp.concatenate([jnp.where(low, part, zero), gate], axis=1),
                jnp.concatenate([jnp.where(low, zero, part), gate], axis=1),
            ],
            axis=0,
        )
        scores = dot_t(queries, jnp.concatenate([keys[:, lanes], gates], axis=1))
        top = jnp.broadcast_to(jnp.max(scores, axis=1, keepdims=True), (2 * rows, LANES))
        if not first:
            before = top_in[index]
            top = jnp.maximum(top, before)
            fade = jnp.exp2(before - top)
            fade = jnp.where(low, fade[:rows], fade[rows:])
        spread_top = jnp.concatenate([top] * (scores.shape[1] // LANES), axis=1)
        weights = jnp.exp2(scores - spread_top).astype(BF16)
        sums = dot(weights, jnp.concatenate([values[:, lanes], ones], axis=1))
        acc = jnp.where(low, sums[:rows, :LANES], sums[rows:, :LANES])
        norm = jnp.where(low, sums[:rows, LANES:], sums[rows:, LANES:])
        if not first:
            acc = acc_in[:, lanes] * fade + acc
            norm = norm_in[:, lanes] * fade + norm
        if last:
            pieces.append((acc / norm).astype(BF16))
        else:
            acc_ref[:, lanes] = acc
            norm_ref[:, lanes] = norm
            top_ref[index] = top
    if not last:
        return
    state = state_in[...] + dot(jnp.concatenate(pieces, axis=1), w_out_ref[layer])
    normed = rms(state, mlp_gain_ref[layer : layer + 1, :].astype(F32)).astype(BF16)
    up_hidden = silu(dot(normed, w_up_ref[layer])).astype(BF16)
    state = state + dot(up_hidden, w_down_ref[layer])
    gain_row = layer + 1 if layer + 1 < LAYERS else 0
    state_ref[...] = state
    normed_ref[...] = rms(state, next_gain_ref[gain_row : gain_row + 1, :].astype(F32)).astype(BF16)


def pick_rows(ids, roles, odd, decoded):
    id_rows = ids.shape[0] // 2
    mesh_rows = decoded.shape[0] // len(roles)
    node, step = ids[:id_rows].astype(F32), ids[id_rows:].astype(F32)
    code = jnp.full(node.shape, -1.0, F32)
    for place, role in enumerate(roles):
        wanted = jnp.asarray(offset_of(role, odd), jnp.int32).astype(F32)
        code = jnp.where(step == wanted, node + float(place * mesh_rows), code)
    code = jnp.transpose(code)
    nodes = lax.broadcasted_iota(jnp.int32, (LANES, decoded.shape[0]), 1).astype(F32)
    hits = [jnp.where(nodes == code[:, row : row + 1], 1.0, 0.0).astype(BF16) for row in range(id_rows)]
    return dot(jnp.concatenate(hits, axis=0), decoded)


def decode_mid_kernel(roles, me_ref, ids_ref, own_ref, pair_ref, near_ref, wide_ref, rows_ref):
    decoded = jnp.concatenate([own_ref[...], pair_ref[...], near_ref[...], wide_ref[...]], axis=0)
    rows_ref[...] = pick_rows(ids_ref[...], roles, parity(me_ref), decoded).astype(BF16)


def decode_last_kernel(me_ref, ids_ref, far_ref, rows_ref, feat_ref, w_dec_ref, w_head_ref, w_final_ref, out_ref):
    rows = pick_rows(ids_ref[...], ("far",), parity(me_ref), far_ref[...]).astype(BF16) + rows_ref[...]
    mix = (feat_ref[...].astype(F32) + dot(rows, w_dec_ref[...])).astype(BF16)
    head_rows = silu(dot(mix, w_head_ref[...])).astype(BF16)
    out_ref[...] = dot(head_rows, w_final_ref[...]).astype(BF16)


def call(name, kernel, outs, flops):
    def run(*operands):
        specs = [pl.BlockSpec(memory_space=pltpu.SMEM)]
        specs += [pl.BlockSpec(memory_space=pltpu.VMEM) for _ in operands[1:]]
        size = sum(o.size * o.dtype.itemsize for o in operands) + sum(
            int(np.prod(o.shape)) * o.dtype.itemsize for o in outs
        )
        return pl.pallas_call(
            kernel,
            out_shape=outs,
            in_specs=specs,
            out_specs=[pl.BlockSpec(memory_space=pltpu.VMEM) for _ in outs],
            cost_estimate=pl.CostEstimate(flops=flops, bytes_accessed=size, transcendentals=0),
            compiler_params=pltpu.CompilerParams(vmem_limit_bytes=KERNEL_VMEM),
            name=name,
        )(*operands)

    return run


def shape(*sizes, dtype=F32):
    return jax.ShapeDtypeStruct(sizes, dtype)


def body(
    grid_in, dest_block, dest_node, neighbour_mask, mesh_embed, w_in, in_bias, w_grid, w_enc, attn_gain, w_query,
    w_key, w_value, w_out, mlp_gain, w_up, w_down, dec_gain, w_dec, w_head, w_final,
):
    block_count = lax.axis_size("block")
    me = lax.axis_index("block").astype(jnp.int32).reshape(1)
    grid_rows, channels = grid_in.shape
    mesh_rows, width = mesh_embed.shape
    out_width = w_final.shape[1]
    head_dim = width // HEADS
    id_rows = grid_rows // LANES
    bias = in_bias.reshape(1, -1)
    decode_gain = dec_gain.reshape(1, -1)

    packed, ids = call(
        "pack",
        functools.partial(pack_kernel, block_count),
        [shape(grid_rows + 2 * id_rows, channels, dtype=BF16), shape(2 * id_rows, channels, dtype=BF16)],
        grid_rows * channels,
    )(me, grid_in, dest_block.reshape(id_rows, LANES), dest_node.reshape(id_rows, LANES))
    pair, near, wide, far = spread(packed)
    sums = [shape(mesh_rows, width), shape(mesh_rows, LANES)]
    block_flops = 2 * grid_rows * width * (channels + mesh_rows)

    def encode(roles, outs):
        return call(
            "encode_" + roles[0], functools.partial(encode_kernel, roles, grid_rows), outs, len(roles) * block_flops
        )

    total, count, feat, gate = encode(
        ("own", "pair"), sums + [shape(grid_rows, width, dtype=BF16), shape(mesh_rows, LANES, dtype=BF16)]
    )(me, packed, pair, w_in, bias, w_grid, neighbour_mask.T)
    total, count = encode(("near", "wide"), sums)(me, near, wide, w_in, bias, total, count)
    states = [shape(mesh_rows, width), shape(mesh_rows, width, dtype=BF16)]
    state, normed = encode(("far",), states)(
        me, far, w_in, bias, total, count, w_grid, w_enc, mesh_embed, attn_gain
    )
    carries = [shape(mesh_rows, width), shape(mesh_rows, width), shape(width // LANES, 2 * mesh_rows, LANES)]
    attend_flops = 4 * mesh_rows * width * (width + mesh_rows)
    for layer in range(LAYERS):

        def attend(roles, outs):
            return call(
                "attend_" + roles[0],
                functools.partial(attend_kernel, roles, layer, head_dim),
                outs,
                len(roles) * attend_flops,
            )

        pair, near, wide, far = spread(normed)
        query, *carry = attend(("own", "pair"), [shape(mesh_rows, width, dtype=BF16)] + carries)(
            me, normed, pair, gate, w_key, w_value, w_query
        )
        carry = attend(("near", "wide"), carries)(me, near, wide, gate, w_key, w_value, query, *carry)
        state, normed = attend(("far",), states)(
            me, far, gate, w_key, w_value, query, *carry, state, w_out, mlp_gain, w_up, w_down,
            attn_gain if layer + 1 < LAYERS else decode_gain,
        )
    pair, near, wide, far = spread(normed)
    (rows,) = call(
        "decode_mid",
        functools.partial(decode_mid_kernel, ("own", "pair", "near", "wide")),
        [shape(grid_rows, width, dtype=BF16)],
        2 * grid_rows * width * 4 * mesh_rows,
    )(me, ids, normed, pair, near, wide)
    (grid_out,) = call(
        "decode_last",
        decode_last_kernel,
        [shape(grid_rows, out_width, dtype=BF16)],
        2 * grid_rows * width * 3 * width,
    )(me, ids, far, rows, feat, w_dec, w_head, w_final)
    return grid_out


def solution(mesh):
    split = P(("member", "block"), None)
    placed = (split, split, P(("member", "block")), split, split) + (P(),) * 16
    return jax.shard_map(body, mesh=mesh, in_specs=placed, out_specs=split, check_vma=False)
```
